128 devices in a mesh: dp: 4 (over x_hi, core), tm: 32 (over x_lo, y, z).
Axes of the slice: x: 4 (x_hi: 2, x_lo: 2; x = x_hi * 2 + x_lo), y: 4, z: 4, core: 2. Of those that a mesh axis runs over, the one named last changes fastest.
Arguments:
- clips: bfloat16 [4, 64, 512, 1152], P('dp', 'tm'), may hold values from -6 to 6
- w_space_qkv: bfloat16 [1152, 3456], P('dp'), may hold values from -0.1875 to 0.1875
- w_space_out: bfloat16 [1152, 1152], P('dp'), may hold values from -1 to 1
- w_time_qkv: bfloat16 [1152, 3456], P('dp'), may hold values from -0.1875 to 0.1875
- w_time_out: bfloat16 [1152, 1152], P('dp'), may hold values from -1 to 1
- space_pattern: int32 [8, 4], replicated, may hold values from 0 to 7, as said below
- time_pattern: int32 [32, 4], replicated, may hold values from 0 to 31, as said below
Outputs:
- layer_out: bfloat16 [4, 64, 512, 1152], P('dp', 'tm')
The draws below stay inside these ranges and needn't reach their ends.
Inputs may be any that keep to these rules, and one draw needn't show every extreme that they name: `space_pattern`: row i starts with i; the other entries are any blocks, repeats allowed. `time_pattern`: row i starts with i; every entry is at most i, repeats allowed.
All inputs are finite; a program needn't handle non-finite values.
Results may differ from the reference program's by a relative error of at most 0.017.
Values may be sent and summed in bfloat16 or wider, within the bound.
A program may use at most 128 MiB of HBM per device.

```python
import jax
import jax.numpy as jnp
from jax import lax

HEADS = 16
HEAD_FEATURES = 72
WIDTH = 1152
PATCHES = 512
BLOCK_PATCHES = 64
SPACE_PICKS = 4
BLOCK_FRAMES = 2
TIME_PICKS = 4
FRAMES = 64
CLIPS = 4
SPACE_BLOCKS = 8
TIME_BLOCKS = 32


def draw_space_pattern(key, part):
    others = jax.random.randint(jax.random.fold_in(key, 17), (SPACE_BLOCKS, SPACE_PICKS - 1), 0, SPACE_BLOCKS)
    own_block = jnp.arange(SPACE_BLOCKS, dtype=jnp.int32)[:, None]
    return jnp.concatenate([own_block, others.astype(jnp.int32)], axis=1)


def draw_time_pattern(key, part):
    upper = jnp.arange(1, TIME_BLOCKS + 1, dtype=jnp.int32)[:, None]
    others = jax.random.randint(jax.random.fold_in(key, 29), (TIME_BLOCKS, TIME_PICKS - 1), 0, upper)
    own_block = jnp.arange(TIME_BLOCKS, dtype=jnp.int32)[:, None]
    return jnp.concatenate([own_block, others.astype(jnp.int32)], axis=1)


def shard_levels(own_key, extent, shards, low, top_value):
    level = 1.0
    for dim, shards_of in shards:
        draws = jax.random.uniform(jax.random.fold_in(jax.random.fold_in(own_key, 6), dim), (shards_of,), jnp.float32, low / len(shards), top_value / len(shards))
        level = level * jnp.repeat(jnp.exp(draws), extent[dim] // shards_of).reshape((-1,) + (1,) * (len(extent) - 1 - dim))
    return level


def bell_draw(key, shape, scale, most, split=(), kind=jnp.bfloat16):
    level = shard_levels(key, shape, split, -0.22, 0.18) if split else 1.0
    entries = jax.random.normal(key, shape, jnp.float32) * scale * level
    return jnp.minimum(jnp.maximum(entries, -most), most).astype(kind)


def setup_inputs(seed: int = 0) -> dict:
    seeds = jax.random.split(jax.random.key(seed), 8)
    return {
        "clips": bell_draw(seeds[0], (CLIPS, FRAMES, PATCHES, WIDTH), 1.0, 6.0, ((0, 4), (1, 32))),
        "w_space_qkv": bell_draw(seeds[1], (WIDTH, 3 * WIDTH), WIDTH ** -0.5, 0.1875, ((0, 4),)),
        "w_space_out": bell_draw(seeds[2], (WIDTH, WIDTH), (WIDTH // 32) ** -0.5, 1.0, ((0, 4),)),
        "w_time_qkv": bell_draw(seeds[3], (WIDTH, 3 * WIDTH), WIDTH ** -0.5, 0.1875, ((0, 4),)),
        "w_time_out": bell_draw(seeds[4], (WIDTH, WIDTH), (WIDTH // 32) ** -0.5, 1.0, ((0, 4),)),
        "space_pattern": draw_space_pattern(jax.random.fold_in(seeds[7], 71), 0),
        "time_pattern": draw_time_pattern(jax.random.fold_in(seeds[7], 71), 0),
    }


def layer_norm(values):
    average = lax.optimization_barrier(jnp.mean(values, axis=-1, keepdims=True))
    centred = values - average
    variance = lax.optimization_barrier(jnp.mean(centred * centred, axis=-1, keepdims=True))
    return centred * lax.rsqrt(variance + 1e-06)

def head_norm(values):
    return values * lax.rsqrt(lax.optimization_barrier(jnp.mean(values * values, axis=-1, keepdims=True)) + 1e-06)

def split_heads(packed):
    width = packed.shape[-1] // 3
    leading = packed.shape[:-1]
    query_part = packed[..., :width].reshape(leading + (HEADS, HEAD_FEATURES))
    key_part = packed[..., width:2 * width].reshape(leading + (HEADS, HEAD_FEATURES))
    value_part = packed[..., 2 * width:].reshape(leading + (HEADS, HEAD_FEATURES))
    query_rows = head_norm(query_part.astype(jnp.float32)).astype(jnp.bfloat16)
    incoming_keys = head_norm(key_part.astype(jnp.float32)).astype(jnp.bfloat16)
    return (query_rows, incoming_keys, value_part)

def block_allowed(pattern, count, repeat):
    hits = pattern[:, :, None] == jnp.arange(count, dtype=jnp.int32)[None, None, :]
    blocks = jnp.any(hits, axis=1)
    return jnp.repeat(jnp.repeat(blocks, repeat, axis=0), repeat, axis=1)

def spatial_attend(packed, allowed):
    query_rows, incoming_keys, incoming_values = split_heads(packed)
    logit_scores = jnp.einsum('pxg,exg->xpe', query_rows.astype(jnp.float32), incoming_keys.astype(jnp.float32)) * HEAD_FEATURES ** (-0.5)
    softmax_weights = jnp.where(allowed[None], jnp.exp(logit_scores), 0.0)
    totals = lax.optimization_barrier(jnp.sum(softmax_weights, axis=-1))
    rounded_scores = lax.optimization_barrier(softmax_weights.astype(jnp.bfloat16)).astype(jnp.float32)
    blended_values = jnp.einsum('fok,kfv->ofv', rounded_scores, incoming_values.astype(jnp.float32))
    blended_values = blended_values / jnp.transpose(totals)[:, :, None]
    return blended_values.reshape(packed.shape[0], -1).astype(jnp.bfloat16)

def temporal_attend(packed, allowed):
    query_rows, incoming_keys, incoming_values = split_heads(packed)
    logit_scores = jnp.einsum('fphd,gphd->phfg', query_rows.astype(jnp.float32), incoming_keys.astype(jnp.float32)) * HEAD_FEATURES ** (-0.5)
    softmax_weights = jnp.where(allowed[None, None], jnp.exp(logit_scores), 0.0)
    totals = lax.optimization_barrier(jnp.sum(softmax_weights, axis=-1))
    rounded_scores = lax.optimization_barrier(softmax_weights.astype(jnp.bfloat16)).astype(jnp.float32)
    blended_values = jnp.einsum('phfg,gphd->fphd', rounded_scores, incoming_values.astype(jnp.float32))
    blended_values = blended_values / jnp.transpose(totals, (2, 0, 1))[..., None]
    return blended_values.reshape(packed.shape[0], packed.shape[1], -1).astype(jnp.bfloat16)

def reference(clips, w_space_qkv, w_space_out, w_time_qkv, w_time_out, space_pattern, time_pattern):
    space_allowed = block_allowed(space_pattern, SPACE_BLOCKS, BLOCK_PATCHES)
    time_allowed = block_allowed(time_pattern, TIME_BLOCKS, BLOCK_FRAMES)

    def frame_attend(frame_rows):
        return spatial_attend(frame_rows, space_allowed)

    def one_clip(clip_rows):
        normed = layer_norm(clip_rows.astype(jnp.float32)).astype(jnp.bfloat16).reshape(FRAMES * PATCHES, WIDTH)
        packed = jnp.dot(normed, w_space_qkv, preferred_element_type=jnp.float32).astype(jnp.bfloat16)
        packed = packed.reshape(FRAMES, PATCHES, 3 * WIDTH)
        attended = lax.map(frame_attend, packed)
        branch = jnp.dot(attended.reshape(FRAMES * PATCHES, WIDTH), w_space_out, preferred_element_type=jnp.float32)
        hidden = (clip_rows.astype(jnp.float32) + branch.reshape(FRAMES, PATCHES, WIDTH)).astype(jnp.bfloat16)
        time_normed = layer_norm(hidden.astype(jnp.float32)).astype(jnp.bfloat16).reshape(FRAMES * PATCHES, WIDTH)
        time_packed = jnp.dot(time_normed, w_time_qkv, preferred_element_type=jnp.float32).astype(jnp.bfloat16)
        time_packed = time_packed.reshape(FRAMES, PATCHES, 3 * WIDTH)
        time_attended = temporal_attend(time_packed, time_allowed)
        time_branch = jnp.dot(time_attended.reshape(FRAMES * PATCHES, WIDTH), w_time_out, preferred_element_type=jnp.float32)
        return (hidden.astype(jnp.float32) + time_branch.reshape(FRAMES, PATCHES, WIDTH)).astype(jnp.bfloat16)
    return lax.map(one_clip, clips)
```

```python
from functools import partial

import jax
import jax.numpy as jnp
from jax import lax
from jax.sharding import PartitionSpec as P

HEADS = 16
HEAD_FEATURES = 72
WIDTH = 1152
PATCHES = 512


def layer_norm(values):
    average = jnp.mean(values, axis=-1, keepdims=True)
    centred = values - average
    variance = jnp.mean(centred * centred, axis=-1, keepdims=True)
    return centred * lax.rsqrt(variance + 1e-06)


def head_norm(values):
    return values * lax.rsqrt(jnp.mean(values * values, axis=-1, keepdims=True) + 1e-06)


def split_heads(packed):
    width = packed.shape[-1] // 3
    leading = packed.shape[:-1]
    query_part = packed[..., :width].reshape(leading + (HEADS, HEAD_FEATURES))
    key_part = packed[..., width : 2 * width].reshape(leading + (HEADS, HEAD_FEATURES))
    value_part = packed[..., 2 * width :].reshape(leading + (HEADS, HEAD_FEATURES))
    query_rows = head_norm(query_part.astype(jnp.float32)).astype(jnp.bfloat16)
    incoming_keys = head_norm(key_part.astype(jnp.float32)).astype(jnp.bfloat16)
    return (query_rows, incoming_keys, value_part)


def block_allowed(pattern, count, repeat):
    hits = pattern[:, :, None] == jnp.arange(count, dtype=jnp.int32)[None, None, :]
    blocks = jnp.any(hits, axis=1)
    return jnp.repeat(jnp.repeat(blocks, repeat, axis=0), repeat, axis=1)


def spatial_attend(allowed, packed):
    query_rows, incoming_keys, incoming_values = split_heads(packed)
    logit_scores = jnp.einsum(
        "pxg,exg->xpe", query_rows, incoming_keys, preferred_element_type=jnp.float32
    ) * HEAD_FEATURES ** (-0.5)
    softmax_weights = jnp.where(allowed[None], jnp.exp(logit_scores), 0.0)
    totals = jnp.sum(softmax_weights, axis=-1)
    blended_values = jnp.einsum(
        "fok,kfv->ofv",
        softmax_weights.astype(jnp.bfloat16),
        incoming_values,
        preferred_element_type=jnp.float32,
    )
    blended_values = blended_values / jnp.transpose(totals)[:, :, None]
    return blended_values.reshape(packed.shape[0], -1).astype(jnp.bfloat16)


def temporal_attend(packed, allowed):
    query_rows, incoming_keys, incoming_values = split_heads(packed)
    logit_scores = jnp.einsum(
        "fphd,gphd->phfg", query_rows, incoming_keys, preferred_element_type=jnp.float32
    ) * HEAD_FEATURES ** (-0.5)
    softmax_weights = jnp.where(allowed[None, None], jnp.exp(logit_scores), 0.0)
    totals = jnp.sum(softmax_weights, axis=-1)
    blended_values = jnp.einsum(
        "phfg,gphd->fphd",
        softmax_weights.astype(jnp.bfloat16),
        incoming_values,
        preferred_element_type=jnp.float32,
    )
    blended_values = blended_values / jnp.transpose(totals, (2, 0, 1))[..., None]
    return blended_values.reshape(packed.shape[0], packed.shape[1], -1).astype(jnp.bfloat16)


def add_rows(inputs, shard_rows):
    return jnp.dot(inputs, shard_rows, preferred_element_type=jnp.float32)


def space_qkv(inputs, weight):
    return add_rows(inputs, lax.all_gather(weight, "dp", axis=0, tiled=True))


def space_out(inputs, weight):
    return add_rows(inputs, lax.all_gather(weight, "dp", axis=0, tiled=True))


def time_qkv(inputs, weight):
    return add_rows(inputs, lax.all_gather(weight, "dp", axis=0, tiled=True))


def time_out(inputs, weight):
    return add_rows(inputs, lax.all_gather(weight, "dp", axis=0, tiled=True))


def shards(clips, w_space_qkv, w_space_out, w_time_qkv, w_time_out, space_pattern, time_pattern):
    frames_dev = clips.shape[1]
    frames_all = frames_dev * lax.axis_size("tm")
    space_allowed = block_allowed(
        space_pattern, space_pattern.shape[0], PATCHES // space_pattern.shape[0]
    )
    time_allowed = block_allowed(
        time_pattern, time_pattern.shape[0], frames_all // time_pattern.shape[0]
    )
    local_rows = frames_dev * PATCHES
    normed = layer_norm(clips.astype(jnp.float32)).astype(jnp.bfloat16).reshape(local_rows, WIDTH)
    packed = (
        space_qkv(normed, w_space_qkv).astype(jnp.bfloat16).reshape(frames_dev, PATCHES, 3 * WIDTH)
    )
    attended = lax.map(partial(spatial_attend, space_allowed), packed)
    branch = space_out(attended.reshape(local_rows, WIDTH), w_space_out)
    hidden = (clips.astype(jnp.float32) + branch.reshape(1, frames_dev, PATCHES, WIDTH)).astype(
        jnp.bfloat16
    )
    moved = lax.all_to_all(hidden, "tm", split_axis=2, concat_axis=1, tiled=True)[0]
    moved_shape = moved.shape
    time_normed = (
        layer_norm(moved.astype(jnp.float32)).astype(jnp.bfloat16).reshape(local_rows, WIDTH)
    )
    time_packed = (
        time_qkv(time_normed, w_time_qkv)
        .astype(jnp.bfloat16)
        .reshape(moved_shape[0], moved_shape[1], 3 * WIDTH)
    )
    time_attended = temporal_attend(time_packed, time_allowed)
    final_branch = time_out(time_attended.reshape(local_rows, WIDTH), w_time_out)
    final = (moved.astype(jnp.float32) + final_branch.reshape(moved_shape)).astype(jnp.bfloat16)
    return lax.all_to_all(final[None], "tm", split_axis=1, concat_axis=2, tiled=True)


def solution(mesh):
    return jax.shard_map(
        shards,
        mesh=mesh,
        in_specs=(
            P("dp", "tm", None, None),
            P("dp", None),
            P("dp", None),
            P("dp", None),
            P("dp", None),
            P(),
            P(),
        ),
        out_specs=P("dp", "tm", None, None),
        check_vma=False,
    )
```
